128 devices in a mesh: polar: 16 (over y_hi, z, core), azimuth: 8 (over y_lo, x).
Axes of the slice: x: 4, y: 4 (y_hi: 2, y_lo: 2; y = y_hi * 2 + y_lo), z: 4, core: 2. Of those that a mesh axis runs over, the one named last changes fastest.
Arguments:
- signal: bfloat16 [1024, 768, 256], P('polar', 'azimuth'), may hold values from -6 to 6
- cotangent: bfloat16 [1024, 768, 256], P('polar', 'azimuth'), may hold values from -6 to 6
- mixing: bfloat16 [2, 256, 256], replicated, may hold values from -0.25 to 0.25
- coupling: bfloat16 [16, 6, 64, 64], replicated, may hold values from -0.75 to 0.75
- filters: float32 [16, 6, 2, 384], P(None, None, None, 'azimuth'), may hold values from -4 to 4
- band_counts: int32 [16], replicated, may hold values from 2 to 6, as said below
- band_offsets: int32 [16, 6], replicated, may hold values from -1 to 1, as said below
- band_basis: int32 [16, 6], replicated, may hold values from 0 to 1
Outputs:
- output: bfloat16 [1024, 768, 256], P('polar', 'azimuth')
- signal_grad: bfloat16 [1024, 768, 256], P('polar', 'azimuth')
The draws below stay inside these ranges and needn't reach their ends.
Inputs may be any that keep to these rules, and one draw needn't show every extreme that they name: `band_counts`: blocks 1 and 14 use all 6 slots; the two end blocks use at most 4. `band_offsets`: for every block b, the first band_counts[b] slots name distinct pairs of offset and basis, and b plus the offset lies in 0 to 15; later slots are unused.
All inputs are finite; a program needn't handle non-finite values.
Results may differ from the reference program's by a relative error of at most 0.0075.
Values may be sent and summed in bfloat16 or wider, within the bound.
No kernel may reach another device: no remote copies, remote signals or barrier semaphores. Data moves between devices by JAX's collectives and lax.ppermute only.
A program may use at most 192 MiB of HBM per device.

```python
import math
import jax
import jax.numpy as jnp
from jax import lax

C = 256
NLON = 768
M = 384
K = 2
BLOCK = 64
SLOTS = 6
NBLK = 16
NLAT = 1024


def band_pattern(key):
    base = jax.random.fold_in(key, 11)
    key_jitter = jax.random.fold_in(base, 1)
    key_border = jax.random.fold_in(base, 2)
    key_pick = jax.random.fold_in(base, 3)
    blocks = jnp.arange(NBLK, dtype=jnp.int32)
    distance = jnp.minimum(blocks, NBLK - 1 - blocks)
    reach_blocks = max(NBLK // 2 - 1, 1)
    jitter = jax.random.randint(key_jitter, (NBLK,), 0, 2 * K + 1, dtype=jnp.int32)
    inner = jnp.clip(3 * K - 2 * K * (distance - 1) // reach_blocks - jitter, K, 3 * K)
    border = jax.random.randint(key_border, (NBLK,), K, 2 * K + 1, dtype=jnp.int32)
    counts = jnp.where(distance == 0, border, jnp.where(distance == 1, 3 * K, inner)).astype(jnp.int32)
    pairs = jnp.arange(3 * K, dtype=jnp.int32)
    offset = pairs // K - 1
    target = blocks[:, None] + offset[None, :]
    valid = (target >= 0) & (target < NBLK)
    score = jax.random.randint(key_pick, (NBLK, 3 * K), 0, 2 ** 20, dtype=jnp.int32) * 64 + pairs[None, :]
    score = jnp.where(valid, score, score + 2 ** 27)
    order = jnp.argsort(score, axis=1).astype(jnp.int32)
    return (counts, (order // K - 1).astype(jnp.int32), (order % K).astype(jnp.int32))


def draw_band_counts(key, part):
    return band_pattern(key)[0]


def draw_band_offsets(key, part):
    return band_pattern(key)[1]


def draw_band_basis(key, part):
    return band_pattern(key)[2]


def shard_levels(stream_key, dims, cuts, least, high):
    def one(dim, blocks):
        heights = jax.random.uniform(jax.random.fold_in(jax.random.fold_in(stream_key, 6), dim), (blocks,), jnp.float32, least / len(cuts), high / len(cuts))
        return jnp.repeat(jnp.exp(heights), dims[dim] // blocks).reshape((-1,) + (1,) * (len(dims) - dim - 1))

    loudness = one(*cuts[0])
    for cut in cuts[1:]:
        loudness = loudness * one(*cut)
    return loudness


def gaussian(stream_key, extent, width, bound, shards=(), kind=jnp.bfloat16):
    entries = width * jax.random.normal(stream_key, extent, jnp.float32)
    if shards:
        entries = entries * shard_levels(stream_key, extent, shards, -0.22, 0.18)
    return jnp.clip(entries, -bound, bound).astype(kind)


def setup_inputs(seed: int = 0) -> dict:
    arg_keys = jax.random.split(jax.random.key(seed), 9)
    signal = gaussian(arg_keys[0], (NLAT, NLON, C), 1.0, 6.0, ((0, 16), (1, 8)))
    cotangent = gaussian(arg_keys[1], (NLAT, NLON, C), 1.0, 6.0, ((0, 16), (1, 8)))
    mixing = gaussian(arg_keys[2], (K, C, C), (C * K) ** -0.5, 0.25)
    coupling = gaussian(arg_keys[3], (NBLK, SLOTS, BLOCK, BLOCK), BLOCK ** -0.5, 0.75)
    filters = gaussian(arg_keys[4], (NBLK, SLOTS, 2, M), 0.7, 4.0, ((3, 8),), jnp.float32)
    band_counts = draw_band_counts(jax.random.fold_in(arg_keys[8], 71), 0)
    band_offsets = draw_band_offsets(jax.random.fold_in(arg_keys[8], 71), 0)
    band_basis = draw_band_basis(jax.random.fold_in(arg_keys[8], 71), 0)
    return dict(signal=signal, cotangent=cotangent, mixing=mixing, coupling=coupling, filters=filters, band_counts=band_counts, band_offsets=band_offsets, band_basis=band_basis)


def spectral_tables():
    longitude = jnp.arange(NLON, dtype=jnp.int32)
    wavenumber = jnp.arange(M, dtype=jnp.int32)
    product_mod = (longitude[:, None] * wavenumber[None, :]) % NLON
    phase_angle = product_mod.astype(jnp.float32) * (2.0 * math.pi / NLON)
    cosine = jnp.cos(phase_angle)
    sine_part = jnp.sin(phase_angle)
    forward = jnp.stack([cosine, -sine_part], axis=1).astype(jnp.bfloat16)
    weight = jnp.where(wavenumber == 0, 1.0, 2.0).astype(jnp.float32) / NLON
    inverse = jnp.transpose(jnp.stack([cosine, -sine_part], axis=0) * weight[None, None, :], (2, 0, 1)).astype(jnp.bfloat16)
    return forward, inverse


def apply_filter(filt, coupled, conjugate):
    real_part = filt[0][:, None, None]
    imag_part = filt[1][:, None, None]
    if conjugate:
        imag_part = -imag_part
    leading = real_part * coupled[:, 0] - imag_part * coupled[:, 1]
    trailing = real_part * coupled[:, 1] + imag_part * coupled[:, 0]
    return jnp.stack([leading, trailing], axis=1)


def reference(signal, cotangent, mixing, coupling, filters, band_counts, band_offsets, band_basis):
    forward, inverse = spectral_tables()
    forward_wide = forward.astype(jnp.float32)
    inverse_wide = inverse.astype(jnp.float32)
    mixing_wide = mixing.astype(jnp.float32)
    signal_blocks = signal.reshape(NBLK, BLOCK, NLON, C)
    cotangent_blocks = cotangent.reshape(NBLK, BLOCK, NLON, C)

    def to_modes(pieces):
        spectra = jnp.einsum('inc,npm->mpic', pieces[0].astype(jnp.float32), forward_wide).astype(jnp.bfloat16)
        gradients = jnp.einsum('inc,mpn->mpic', pieces[1].astype(jnp.float32), inverse_wide).astype(jnp.bfloat16)
        return spectra, gradients

    spectra, gradients = lax.map(to_modes, (signal_blocks, cotangent_blocks))
    border = jnp.zeros((1,) + spectra.shape[1:], jnp.bfloat16)
    spectra = jnp.concatenate([border, spectra, border], 0)
    gradients = jnp.concatenate([border, gradients, border], 0)
    zero_totals = jnp.zeros((K, M, 2, BLOCK, C), jnp.float32)

    def forward_block(block):
        def add_slot(slot, totals):
            offset = band_offsets[block, slot]
            basis = band_basis[block, slot]
            source = lax.dynamic_index_in_dim(spectra, block + offset + 1, 0, keepdims=False).astype(jnp.float32)
            coupled = jnp.einsum('rj,mpjc->mprc', coupling[block, slot].astype(jnp.float32), source)
            filtered = apply_filter(filters[block, slot], coupled, False)
            current = lax.dynamic_index_in_dim(totals, basis, 0, keepdims=False)
            return lax.dynamic_update_index_in_dim(totals, current + filtered, basis, 0)

        totals = lax.fori_loop(0, band_counts[block], add_slot, zero_totals)
        rounded = totals.astype(jnp.bfloat16).astype(jnp.float32)
        out_spectra = jnp.einsum('kmpic,kcd->mpid', rounded, mixing_wide).astype(jnp.bfloat16)
        return jnp.einsum('mpic,mpn->inc', out_spectra.astype(jnp.float32), inverse_wide).astype(jnp.bfloat16)

    def backward_block(block):
        totals = zero_totals
        for step_by in (-1, 0, 1):
            neighbour = block + step_by
            inside = (neighbour >= 0) & (neighbour < NBLK)
            safe = jnp.clip(neighbour, 0, NBLK - 1).astype(jnp.int32)
            source = lax.dynamic_index_in_dim(gradients, block + step_by + 1, 0, keepdims=False).astype(jnp.float32)
            count_there = band_counts[safe]

            def add_slot(slot, totals, safe=safe, inside=inside, source=source, count_there=count_there, step_by=step_by):
                used = inside & (slot < count_there) & (band_offsets[safe, slot] == -step_by)
                basis = band_basis[safe, slot]

                def update(totals):
                    lifted = jnp.einsum('jr,mpjc->mprc', coupling[safe, slot].astype(jnp.float32), source)
                    filtered = apply_filter(filters[safe, slot], lifted, True)
                    current = lax.dynamic_index_in_dim(totals, basis, 0, keepdims=False)
                    return lax.dynamic_update_index_in_dim(totals, current + filtered, basis, 0)

                return lax.cond(used, update, lambda kept: kept, totals)

            totals = lax.fori_loop(0, SLOTS, add_slot, totals)
        rounded = totals.astype(jnp.bfloat16).astype(jnp.float32)
        grad_spectra = jnp.einsum('kmpjd,kcd->mpjc', rounded, mixing_wide).astype(jnp.bfloat16)
        return jnp.einsum('mpjc,npm->jnc', grad_spectra.astype(jnp.float32), forward_wide).astype(jnp.bfloat16)

    block_ids = jnp.arange(NBLK, dtype=jnp.int32)
    output = lax.map(forward_block, block_ids).reshape(NLAT, NLON, C)
    signal_grad = lax.map(backward_block, block_ids).reshape(NLAT, NLON, C)
    return output, signal_grad
```

```python
import math

import jax
import jax.numpy as jnp
from jax import lax
from jax.experimental import pallas as pl
from jax.experimental.pallas import tpu as pltpu
from jax.sharding import PartitionSpec as P

NLON = 768
M = 384
K = 2
BLOCK = 64
PARTS = 8
LON = NLON // PARTS
CHANNELS = 256
SUB = 16
HALVES = 2
TILES = BLOCK // SUB
F32 = jnp.float32
BF16 = jnp.bfloat16


def spectral_tables():
    longitude = jnp.arange(NLON, dtype=jnp.int32)
    wavenumber = jnp.arange(M, dtype=jnp.int32)
    product_mod = wavenumber[:, None] * longitude[None, :] % NLON
    phase_angle = product_mod.astype(F32) * (2.0 * math.pi / NLON)
    table = jnp.concatenate([jnp.cos(phase_angle), -jnp.sin(phase_angle)], axis=0)
    weight = jnp.where(wavenumber == 0, 1.0, 2.0).astype(F32) / NLON
    weight = jnp.concatenate([weight, weight])
    forward = table.astype(BF16)
    inverse = (table * weight[:, None]).astype(BF16)
    return forward, inverse


def swap_order():
    index = jnp.arange(SUB * SUB, dtype=jnp.int32)
    partner = index % SUB * SUB + index // SUB
    return (index[None, :] == partner[:, None]).astype(BF16)


def butterfly(parts):
    parts = list(parts)
    lane = lax.broadcasted_iota(jnp.int32, parts[0].shape, 1)
    for bit in (1, 2, 4):
        shift = SUB * bit
        low = (lane & shift) == 0
        for place in range(8):
            if place & bit:
                continue
            first, second = parts[place], parts[place | bit]
            parts[place] = jnp.where(low, first, pltpu.roll(second, shift, 1))
            parts[place | bit] = jnp.where(low, pltpu.roll(first, 128 - shift, 1), second)
    return parts


def pack_kernel(x_ref, *out_refs):
    for v in range(2):
        for w in range(2):
            moved = butterfly(
                [x_ref[8 * w + e, :, 128 * v : 128 * v + 128].astype(F32) for e in range(8)]
            )
            for place in range(8):
                group = 8 * v + place
                out_refs[group % 2][group // 2, 0, :, 128 * w : 128 * w + 128] = moved[
                    place
                ].astype(BF16)


def pack(x):
    step = 32
    return pl.pallas_call(
        pack_kernel,
        grid=(TILES, LON // step),
        in_specs=[pl.BlockSpec((SUB, step, CHANNELS), lambda t, n: (t, n, 0))],
        out_specs=[
            pl.BlockSpec((PARTS, 1, step, CHANNELS), lambda t, n: (0, t, n, 0))
            for _ in range(HALVES)
        ],
        out_shape=[
            jax.ShapeDtypeStruct((PARTS, TILES, LON, CHANNELS), BF16) for _ in range(HALVES)
        ],
        cost_estimate=pl.CostEstimate(flops=0, bytes_accessed=6_300_000, transcendentals=0),
        name="pack",
    )(x)


def to_modes_kernel(t_ref, p_ref, x_ref, o_ref):
    x = x_ref[...].reshape(NLON, CHANNELS)
    spectra = jnp.dot(t_ref[...], x, preferred_element_type=F32).astype(BF16)
    turned = lax.dot_general(
        p_ref[...], spectra, (((1,), (1,)), ((), ())), preferred_element_type=F32
    )
    o_ref[...] = turned.astype(BF16).reshape(SUB, SUB, NLON)


def to_modes(table, order, x):
    return pl.pallas_call(
        to_modes_kernel,
        grid=(TILES,),
        in_specs=[
            pl.BlockSpec((NLON, NLON), lambda t: (0, 0)),
            pl.BlockSpec((SUB * SUB, SUB * SUB), lambda t: (0, 0)),
            pl.BlockSpec((PARTS, 1, LON, CHANNELS), lambda t: (0, t, 0, 0)),
        ],
        out_specs=pl.BlockSpec((SUB, SUB, NLON), lambda t: (0, t, 0)),
        out_shape=jax.ShapeDtypeStruct((SUB, BLOCK, NLON), BF16),
        cost_estimate=pl.CostEstimate(
            flops=2 * NLON * NLON * 1024, bytes_accessed=4_500_000, transcendentals=0
        ),
        name="to_modes",
    )(table, order, x)


def couple_kernel(a_ref, f_ref, l_ref, m_ref, r_ref, o_ref):
    for c in range(m_ref.shape[0]):
        for start in range(0, M, 128):
            real = [None] * K
            imag = [None] * K
            for side, s_ref in enumerate((l_ref, m_ref, r_ref)):
                source = jnp.concatenate(
                    [
                        s_ref[c, :, start : start + 128],
                        s_ref[c, :, M + start : M + start + 128],
                    ],
                    axis=1,
                )
                mixed = jnp.dot(a_ref[side], source, preferred_element_type=F32)
                for k in range(K):
                    row = 2 * (3 * k + side)
                    f_real = f_ref[row : row + 1, start : start + 128]
                    f_imag = f_ref[row + 1 : row + 2, start : start + 128]
                    c_real = mixed[BLOCK * k : BLOCK * (k + 1), :128]
                    c_imag = mixed[BLOCK * k : BLOCK * (k + 1), 128:]
                    t_real = f_real * c_real - f_imag * c_imag
                    t_imag = f_real * c_imag + f_imag * c_real
                    real[k] = t_real if side == 0 else real[k] + t_real
                    imag[k] = t_imag if side == 0 else imag[k] + t_imag
            for k in range(K):
                o_ref[k, c, :, start : start + 128] = real[k].astype(BF16)
                o_ref[k, c, :, M + start : M + start + 128] = imag[k].astype(BF16)


def couple(maps, filters, left, own, right):
    step = 4
    spec = pl.BlockSpec((step, BLOCK, NLON), lambda c: (c, 0, 0))
    return pl.pallas_call(
        couple_kernel,
        grid=(SUB // step,),
        in_specs=[
            pl.BlockSpec((3, K * BLOCK, BLOCK), lambda c: (0, 0, 0)),
            pl.BlockSpec((12, M), lambda c: (0, 0)),
            spec,
            spec,
            spec,
        ],
        out_specs=pl.BlockSpec((K, step, BLOCK, NLON), lambda c: (0, c, 0, 0)),
        out_shape=jax.ShapeDtypeStruct((K, SUB, BLOCK, NLON), BF16),
        cost_estimate=pl.CostEstimate(
            flops=4 * 2 * 3 * SUB * 128 * BLOCK * NLON,
            bytes_accessed=8_000_000,
            transcendentals=0,
        ),
        name="couple",
    )(maps, filters, left, own, right)


def to_longitudes_kernel(t_ref, p_ref, b_ref, o_ref):
    sums = b_ref[...].reshape(SUB * SUB, NLON)
    grid = lax.dot_general(
        t_ref[...], sums, (((1,), (1,)), ((), ())), preferred_element_type=F32
    ).astype(BF16)
    turned = jnp.dot(grid, p_ref[...], preferred_element_type=F32).astype(BF16)
    o_ref[...] = turned.reshape(PARTS, 1, 1, LON, CHANNELS)


def to_longitudes(table, order, sums):
    return pl.pallas_call(
        to_longitudes_kernel,
        grid=(K, TILES),
        in_specs=[
            pl.BlockSpec((NLON, NLON), lambda k, t: (0, 0)),
            pl.BlockSpec((SUB * SUB, SUB * SUB), lambda k, t: (0, 0)),
            pl.BlockSpec((1, SUB, SUB, NLON), lambda k, t: (k, 0, t, 0)),
        ],
        out_specs=pl.BlockSpec((PARTS, 1, 1, LON, CHANNELS), lambda k, t: (0, k, t, 0, 0)),
        out_shape=jax.ShapeDtypeStruct((PARTS, K, TILES, LON, CHANNELS), BF16),
        cost_estimate=pl.CostEstimate(
            flops=2 * NLON * NLON * 2048, bytes_accessed=7_500_000, transcendentals=0
        ),
        name="to_longitudes",
    )(table, order, sums)


def mix_kernel(turn, w_ref, *refs):
    halves, o_ref = refs[:-1], refs[-1]
    step = o_ref.shape[1]
    total = None
    for k in range(K):
        rows = [[None, None] for _ in range(SUB)]
        for v in range(2):
            for w in range(2):
                moved = butterfly(
                    [
                        halves[(8 * v + place) % 2][
                            (8 * v + place) // 2, k, 0, :, 128 * w : 128 * w + 128
                        ].astype(F32)
                        for place in range(8)
                    ]
                )
                for e in range(8):
                    rows[8 * w + e][v] = moved[e].astype(BF16)
        x = jnp.concatenate([jnp.concatenate(row, axis=1) for row in rows], axis=0)
        term = lax.dot_general(
            x, w_ref[k], (((1,), (1 if turn else 0,)), ((), ())), preferred_element_type=F32
        )
        total = term if total is None else total + term
    o_ref[...] = total.astype(BF16).reshape(SUB, step, CHANNELS)


def mix(mixing, halves, turn):
    step = 32
    return pl.pallas_call(
        lambda *refs: mix_kernel(turn, *refs),
        grid=(TILES, LON // step),
        in_specs=[pl.BlockSpec((K, CHANNELS, CHANNELS), lambda t, n: (0, 0, 0))]
        + [
            pl.BlockSpec((PARTS, K, 1, step, CHANNELS), lambda t, n: (0, 0, t, n, 0))
            for _ in range(HALVES)
        ],
        out_specs=pl.BlockSpec((SUB, step, CHANNELS), lambda t, n: (t, n, 0)),
        out_shape=jax.ShapeDtypeStruct((BLOCK, LON, CHANNELS), BF16),
        cost_estimate=pl.CostEstimate(
            flops=2 * 64 * 96 * 512 * 256, bytes_accessed=9_500_000, transcendentals=0
        ),
        name="mix",
    )(mixing, *halves)


def exchange(x):
    return lax.all_to_all(x, "azimuth", split_axis=0, concat_axis=0, tiled=True)


def neighbours(x):
    count = lax.axis_size("polar")
    return (
        lax.ppermute(x, "polar", [(i, i + 1) for i in range(count - 1)]),
        lax.ppermute(x, "polar", [(i + 1, i) for i in range(count - 1)]),
    )


def dense_tables(coupling, filters, band_counts, band_offsets, band_basis):
    blocks = lax.axis_size("polar")
    own = lax.axis_index("polar")
    slots = coupling.shape[1]
    maps = {}
    gains = {}
    for step in (-1, 0, 1):
        there = own + step
        inside = (there >= 0) & (there < blocks)
        safe = jnp.clip(there, 0, blocks - 1)
        used = inside & (jnp.arange(slots) < band_counts[safe])
        for k in range(K):
            for offset in (-1, 0, 1):
                if step != 0 and offset != -step:
                    continue
                pick = used & (band_offsets[safe] == offset) & (band_basis[safe] == k)
                maps[step, k, offset] = jnp.sum(
                    jnp.where(pick[:, None, None], coupling[safe], 0).astype(F32), axis=0
                ).astype(BF16)
                gains[step, k, offset] = jnp.sum(
                    jnp.where(pick[:, None, None], filters[safe], 0.0), axis=0
                )
    ahead_maps = jnp.stack(
        [jnp.concatenate([maps[0, k, o] for k in range(K)], axis=0) for o in (-1, 0, 1)]
    )
    back_maps = jnp.stack(
        [jnp.concatenate([maps[s, k, -s].T for k in range(K)], axis=0) for s in (-1, 0, 1)]
    )
    ahead = jnp.stack([gains[0, k, o] for k in range(K) for o in (-1, 0, 1)])
    back = jnp.stack([gains[s, k, -s] for k in range(K) for s in (-1, 0, 1)])
    back = back * jnp.array([1.0, -1.0], F32)[None, :, None]
    local = jnp.concatenate([ahead, back]).reshape(1, 9, 128)
    every = exchange(jnp.broadcast_to(local, (PARTS, 9, 128)))
    every = every.reshape(PARTS, 24, M // PARTS).transpose(1, 0, 2).reshape(24, M)
    return ahead_maps, back_maps, every[:12], every[12:]


def per_device(signal, cotangent, mixing, coupling, filters, band_counts, band_offsets, band_basis):
    forward, inverse = spectral_tables()
    order = swap_order()
    ahead_maps, back_maps, ahead_gain, back_gain = dense_tables(
        coupling, filters, band_counts, band_offsets, band_basis
    )
    arrived = []
    for x in (signal, cotangent):
        arrived.append([exchange(part) for part in pack(x)])
    results = []
    for parts, table, back_table, maps, gain, turn in (
        (arrived[0], forward, inverse.T, ahead_maps, ahead_gain, False),
        (arrived[1], inverse, forward.T, back_maps, back_gain, True),
    ):
        returned = []
        for part in parts:
            spectra = to_modes(table, order, part)
            left, right = neighbours(spectra)
            sums = couple(maps, gain, left, spectra, right)
            returned.append(exchange(to_longitudes(back_table, order, sums)))
        results.append(mix(mixing, returned, turn))
    return tuple(results)


def solution(mesh):
    return jax.shard_map(
        per_device,
        mesh=mesh,
        in_specs=(
            P("polar", "azimuth", None),
            P("polar", "azimuth", None),
            P(),
            P(),
            P(None, None, None, "azimuth"),
            P(),
            P(),
            P(),
        ),
        out_specs=(P("polar", "azimuth", None), P("polar", "azimuth", None)),
        check_vma=False,
    )
```
